32 devices in a mesh: pair: 4 (over y, x), vtile: 8 (over z, core).
Axes of the slice: x: 2, y: 2, z: 4, core: 2. Of those that a mesh axis runs over, the one named last changes fastest.
Arguments:
- amplitudes: bfloat16 [32, 512, 512], P(('pair', 'vtile')), may hold values from -1.1953125 to 1.1953125
- factors: bfloat16 [512, 512, 2048], P('vtile', 'pair'), may hold values from -0.125 to 0.125
- pair_list: int32 [32, 2], P(('pair', 'vtile')), may hold values from 0 to 127
- window_offsets: int32 [2], replicated, may hold values from 0 to 511
- occupied_energy: float32 [128], replicated, may hold values from -3 to -0.5
- virtual_energy: float32 [512], replicated, may hold values from 0.5 to 4
Outputs:
- residual: float32 [32, 2, 512], P(('pair', 'vtile'))
- update: float32 [32, 2, 512], P(('pair', 'vtile'))
The draws below stay inside these ranges and needn't reach their ends.
All inputs are finite; a program needn't handle non-finite values.
Results may differ from the reference program's by a relative error of at most 0.0029.
Values may be sent and summed in bfloat16 or wider, within the bound.
A program may use at most 128 MiB of HBM per device.

```python
import math
import jax
import jax.numpy as jnp
from jax import lax

OCC = 128
VIRT = 512
AUX = 2048
AWIN = 2
PAIRS = 32


def with_ends(entries, stream_key, low, largest):
    spot = [jax.random.randint(jax.random.fold_in(stream_key, axis), (), 0, length) for axis, length in enumerate(entries.shape)]
    widest = entries.shape.index(max(entries.shape))
    next_to = spot[:widest] + [(spot[widest] + 1) % entries.shape[widest]] + spot[widest + 1:]
    return entries.at[tuple(spot)].set(low).at[tuple(next_to)].set(largest)


def shard_levels(own_key, dims, cuts, least, top_value):
    factor_of = 1.0
    for position, parts in cuts:
        heights = jax.random.uniform(jax.random.fold_in(jax.random.fold_in(own_key, 6), position), (parts,), jnp.float32, least / len(cuts), top_value / len(cuts))
        factor_of = factor_of * jnp.repeat(jnp.exp(heights), dims[position] // parts).reshape((-1,) + (1,) * (len(dims) - 1 - position))
    return factor_of


def gaussian(own_key, dims, spread, reach, cuts=(), kind=jnp.bfloat16):
    factor_of = shard_levels(own_key, dims, cuts, -0.22, 0.18) if cuts else 1.0
    drawn = jax.random.normal(own_key, dims, jnp.float32) * spread * factor_of
    return jnp.minimum(jnp.maximum(drawn, -reach), reach).astype(kind)


def setup_inputs(seed: int = 0) -> dict:
    arg_keys = jax.random.split(jax.random.key(seed), 7)
    return {
        "amplitudes": gaussian(arg_keys[0], (PAIRS, VIRT, VIRT), 0.2, 1.1953125, ((0, 32),)),
        "factors": gaussian(arg_keys[1], (VIRT, VIRT, AUX), AUX ** -0.5, 0.125, ((0, 8), (1, 4))),
        "pair_list": with_ends(jax.random.randint(arg_keys[2], (PAIRS, 2), 0, OCC), jax.random.fold_in(arg_keys[2], 1), 0, OCC - 1).astype(jnp.int32),
        "window_offsets": jax.random.randint(arg_keys[3], (AWIN,), 0, VIRT).astype(jnp.int32),
        "occupied_energy": jnp.clip(jax.random.uniform(arg_keys[4], (OCC,), jnp.float32, -3.0, -0.5), -3.0, -0.5),
        "virtual_energy": jnp.clip(jnp.exp(jax.random.uniform(arg_keys[5], (VIRT,), jnp.float32, math.log(0.5), math.log(4.0))), 0.5, 4.0),
    }


def reference(amplitudes, factors, pair_list, window_offsets, occupied_energy, virtual_energy):
    width = min(64, VIRT)
    arows = factors[window_offsets]
    left_side = arows.reshape(AWIN * VIRT, AUX)

    def one_range(range_index):
        offset = (range_index * width).astype(jnp.int32)
        slab = lax.dynamic_slice_in_dim(factors, offset, width, 1)
        integrals = jnp.dot(left_side, slab.reshape(VIRT * width, AUX).T, preferred_element_type=jnp.float32).astype(jnp.bfloat16)
        integrals = integrals.reshape(AWIN, VIRT, VIRT, width).transpose(0, 2, 1, 3).reshape(AWIN * VIRT, VIRT * width)
        tau_slab = lax.dynamic_slice_in_dim(amplitudes, offset, width, 2).reshape(PAIRS, VIRT * width)
        return jnp.dot(tau_slab, integrals.T, preferred_element_type=jnp.float32)

    pieces = lax.map(one_range, jnp.arange(VIRT // width, dtype=jnp.int32))
    residual = jnp.sum(pieces, axis=0).reshape(PAIRS, AWIN, VIRT)
    occupied_sum = occupied_energy[pair_list[:, 0]] + occupied_energy[pair_list[:, 1]]
    window_energy = virtual_energy[window_offsets]
    denominator = window_energy[None, :, None] + virtual_energy[None, None, :] - occupied_sum[:, None, None]
    update = residual / denominator
    return residual, update
```

```python
import functools

import jax
import jax.numpy as jnp
from jax import lax
from jax.experimental import pallas as pl
from jax.experimental.pallas import tpu as pltpu
from jax.sharding import PartitionSpec as P

MESH = pl.DeviceIdType.MESH
VMEM = pl.BlockSpec(memory_space=pltpu.VMEM)
SMEM = pl.BlockSpec(memory_space=pltpu.SMEM)
F32 = jnp.float32
GROUP = 16


def prepare_kernel(
    offsets_ref, pairs_ref, occupied_ref, energy_ref, virtual_ref, factors_ref, amp_ref,
    rows_ref, turned_ref, den_ref, sems,
):
    t = lax.axis_index("vtile")
    row_count = factors_ref.shape[0]
    window = rows_ref.shape[0]

    def local_row(k):
        return offsets_ref[k] - t * row_count

    def pick(k):
        row = jnp.clip(local_row(k), 0, row_count - 1)
        return pltpu.make_async_copy(factors_ref.at[row], rows_ref.at[k], sems.at[k])

    for k in range(window):
        pick(k).start()
    for pair in range(amp_ref.shape[0]):
        turned_ref[pair] = amp_ref[pair].T
        occupied = occupied_ref[pairs_ref[pair, 0]] + occupied_ref[pairs_ref[pair, 1]]
        for k in range(window):
            den_ref[pair, k : k + 1, :] = (energy_ref[offsets_ref[k]] + virtual_ref[...]) - occupied
    for k in range(window):
        pick(k).wait()
        row = local_row(k)

        @pl.when(jnp.logical_or(row < 0, row >= row_count))
        def _():
            rows_ref[k] = jnp.zeros(rows_ref.shape[1:], rows_ref.dtype)


def prepare(amplitudes, factors, pair_list, window_offsets, occupied_energy, virtual_energy):
    local_pairs, virt, _ = amplitudes.shape
    window = window_offsets.shape[0]
    return pl.pallas_call(
        prepare_kernel,
        out_shape=(
            jax.ShapeDtypeStruct((window,) + factors.shape[1:], factors.dtype),
            jax.ShapeDtypeStruct(amplitudes.shape, amplitudes.dtype),
            jax.ShapeDtypeStruct((local_pairs, window, virt), F32),
        ),
        in_specs=[SMEM, SMEM, SMEM, SMEM, VMEM, pl.BlockSpec(memory_space=pl.ANY), VMEM],
        out_specs=(VMEM, VMEM, VMEM),
        scratch_shapes=[pltpu.SemaphoreType.DMA((window,))],
    )(
        window_offsets, pair_list, occupied_energy, virtual_energy,
        virtual_energy.reshape(1, virt), factors, amplitudes,
    )


def ladder_kernel(
    pair_count, tile_count, sub, width,
    rows_ref, turned_ref, den_ref, factors_ref,
    res_ref, upd_ref, land_ref,
    full, core_buf, own_buf, up_buf, down_buf, up_out, down_out,
    taus, sorted_taus, stage_buf, table, swap, half_made, acc, part, inbox,
    core_sems, up_sems, down_sems, peer_sems,
    plane_sems, direct_sems, arrive_sems, relay_sems, mate_sems,
    slab_sems, stage_sems, settle_sems, local_sems,
):
    p = lax.axis_index("pair")
    t = lax.axis_index("vtile")
    core = lax.rem(t, 2)
    stage = t // 2
    stages = tile_count // 2
    total = pair_count * tile_count
    me = p * tile_count + t
    window, cols, aux = rows_ref.shape
    half = aux // 2
    own_b, own_d, _ = factors_ref.shape
    both_b = 2 * own_b
    local_pairs = turned_ref.shape[0]
    block = pair_count * local_pairs
    pairs = tile_count * block
    steps = own_d // GROUP
    spread = swap.shape[0]
    mate = (p, stage * 2 + (1 - core))
    above = (p, t + 2)
    below = (p, t - 2)
    relayed = pair_count == 4
    if relayed:
        across = p + 1 - 2 * lax.rem(p, 2)
        along = lax.rem(p + 2, 4)
        sources = [across, along, lax.rem(across + 2, 4)]
        peers = [(source, t) for source in sources]
    else:
        peers = [(lax.rem(p + j, pair_count), t) for j in range(1, pair_count)]
        sources = [lax.rem(p + pair_count - j, pair_count) for j in range(1, pair_count)]
    near = 2 if relayed else pair_count - 1

    def place(offset):
        other = lax.rem(me + offset, total)
        return other // tile_count, lax.rem(other, tile_count)

    barrier = pltpu.get_barrier_semaphore()
    for offset in range(1, total):
        pl.semaphore_signal(barrier, inc=1, device_id=place(offset), device_id_type=MESH)
    pl.semaphore_wait(barrier, total - 1)

    mine_lanes = pl.ds(pl.multiple_of(core * half, half), half)
    mate_lanes = pl.ds(pl.multiple_of((1 - core) * half, half), half)
    chunks = [(k, pl.ds(s * sub, sub)) for k in range(window) for s in range(cols // sub)]
    count = len(chunks)

    def remote(src, dst, sems, index, device):
        return pltpu.make_async_remote_copy(
            src_ref=src, dst_ref=dst, send_sem=sems.at[(0,) + index], recv_sem=sems.at[(1,) + index],
            device_id=device, device_id_type=MESH,
        )

    def group(i):
        return pl.ds(pl.multiple_of(i * GROUP, GROUP), GROUP)

    def core_copy(h):
        k, rows = chunks[h]
        return remote(rows_ref.at[k, rows, mate_lanes], core_buf.at[k, rows], core_sems, (h,), mate)

    def up_copy(h):
        k, rows = chunks[h]
        return remote(up_out.at[k, rows], up_buf.at[k, rows], up_sems, (h,), above)

    def down_copy(h):
        k, rows = chunks[h]
        return remote(down_out.at[k, rows], down_buf.at[k, rows], down_sems, (h,), below)

    def peer_copy(h, j):
        k, rows = chunks[h]
        if j >= near:
            spot = full.at[k, sources[h % 2], rows]
            return remote(spot, spot, peer_sems, (j, h), peers[1 - h % 2])
        spot = full.at[k, p, rows]
        return remote(spot, spot, peer_sems, (j, h), peers[j])

    def plane_copy(j):
        rows = pl.ds(pl.multiple_of(peers[j][0] * own_d, own_d), own_d)
        spot = taus.at[pl.ds((t * pair_count + p) * local_pairs, local_pairs)]
        return remote(turned_ref.at[:, rows], spot, plane_sems, (j,), peers[j])

    def plane_keep():
        rows = pl.ds(pl.multiple_of(p * own_d, own_d), own_d)
        spot = taus.at[pl.ds((t * pair_count + p) * local_pairs, local_pairs)]
        return pltpu.make_async_copy(turned_ref.at[:, rows], spot, local_sems.at[0])

    def tau_spot(tile, i):
        return taus.at[pl.ds(tile * block, block), group(i)]

    shifts = [shift for shift in (-2, -1, 1, 2) if abs(shift) < stages]

    def in_range(shift):
        return jnp.logical_and(stage + shift >= 0, stage + shift < stages)

    def direct_copy(d, i):
        return pltpu.make_async_remote_copy(
            src_ref=tau_spot(t, i), dst_ref=tau_spot(t, i),
            send_sem=direct_sems.at[d, i], recv_sem=arrive_sems.at[stage, i],
            device_id=(p, t + 2 * shifts[d]), device_id_type=MESH,
        )

    def relay_copy(source, i, shift):
        spot = tau_spot(2 * source + core, i)
        return pltpu.make_async_remote_copy(
            src_ref=spot, dst_ref=spot,
            send_sem=relay_sems.at[source, i], recv_sem=arrive_sems.at[source, i],
            device_id=(p, t + 2 * shift), device_id_type=MESH,
        )

    def mate_copy(source, i):
        spot = tau_spot(2 * source + core, i)
        return remote(spot, spot, mate_sems, (source, i), mate)

    def goes_up(source):
        return jnp.logical_and(stage >= source + 2, stage + 1 < stages)

    def goes_down(source):
        return jnp.logical_and(stage <= source - 2, stage >= 1)

    def send_own(i):
        for d, shift in enumerate(shifts):
            @pl.when(in_range(shift))
            def _():
                direct_copy(d, i).start()

    def relay(i):
        for source in range(stages):
            @pl.when(goes_up(source))
            def _():
                relay_copy(source, i, 1).wait_recv()
                relay_copy(source, i, 1).start()

            @pl.when(goes_down(source))
            def _():
                relay_copy(source, i, -1).wait_recv()
                relay_copy(source, i, -1).start()

    def collect(i):
        for source in range(stages):
            passed = jnp.logical_or(goes_up(source), goes_down(source))

            @pl.when(jnp.logical_not(jnp.logical_or(passed, stage == source)))
            def _():
                relay_copy(source, i, 1).wait_recv()

            mate_copy(source, i).start()

    def slab_copy(i):
        return remote(
            factors_ref.at[:, group(i), mate_lanes], land_ref.at[:, group(i)], slab_sems, (i,), mate
        )

    slots = stage_buf.shape[0]

    def own_load(i, slot):
        return pltpu.make_async_copy(
            factors_ref.at[:, group(i), mine_lanes], stage_buf.at[slot], stage_sems.at[slot]
        )

    def mate_load(i, slot):
        return pltpu.make_async_copy(land_ref.at[:, group(i)], stage_buf.at[slot], stage_sems.at[slot])

    def sort_slab(i, slot, side):
        def one(b, carry):
            rows = stage_buf[slot, group(b)].reshape(GROUP * GROUP, half)
            made = jnp.dot(swap[...], rows, preferred_element_type=F32).astype(table.dtype)
            spot = pl.ds(pl.multiple_of(side * own_b + b * GROUP, GROUP), GROUP)
            table[group(i), spot, :] = made.reshape(GROUP, GROUP, half)
            return carry

        lax.fori_loop(0, own_b // GROUP, one, 0)

    def load_slab(n):
        if n < steps:
            own_load(n, n % slots).start()
        else:
            slab_copy(n - steps).wait_recv()
            mate_load(n - steps, n % slots).start()

    def finish_slab(n):
        if n < steps:
            own_load(n, n % slots).wait()
            sort_slab(n, n % slots, core)
        else:
            mate_load(n - steps, n % slots).wait()
            sort_slab(n - steps, n % slots, 1 - core)

    first = steps + steps // 2
    early_slabs = steps - steps // 2 + 1

    for h in range(count):
        core_copy(h).start()
    for j in range(pair_count - 1):
        plane_copy(j).start()
    plane_keep().start()
    for i in range(min(early_slabs, steps)):
        slab_copy(i).start()
    for n in range(slots - 1):
        load_slab(n)
    lanes = lax.broadcasted_iota(jnp.int32, (spread, spread), 1)
    lines = lax.broadcasted_iota(jnp.int32, (spread, spread), 0)
    swap[...] = jnp.where(
        jnp.logical_and(lines // GROUP == lanes % GROUP, lines % GROUP == lanes // GROUP), 1.0, 0.0
    ).astype(swap.dtype)
    acc[...] = jnp.zeros_like(acc)

    def combine(h):
        k, rows = chunks[h]
        core_copy(h).wait_recv()
        own_buf[k, rows, :] = rows_ref[k, rows, mine_lanes] + core_buf[k, rows, :]

        @pl.when(stage == 0)
        def _():
            up_out[k, rows, :] = own_buf[k, rows, :]
            up_copy(h).start()

        @pl.when(stage == stages - 1)
        def _():
            down_out[k, rows, :] = own_buf[k, rows, :]
            down_copy(h).start()

    def go_up(h):
        k, rows = chunks[h]

        @pl.when(stage > 0)
        def _():
            up_copy(h).wait_recv()

            @pl.when(stage < stages - 1)
            def _():
                up_out[k, rows, :] = own_buf[k, rows, :] + up_buf[k, rows, :]
                up_copy(h).start()

    def go_down(h):
        k, rows = chunks[h]

        @pl.when(stage < stages - 1)
        def _():
            down_copy(h).wait_recv()

            @pl.when(stage > 0)
            def _():
                down_out[k, rows, :] = own_buf[k, rows, :] + down_buf[k, rows, :]
                down_copy(h).start()

    def finish(h):
        k, rows = chunks[h]

        @pl.when(stage == 0)
        def _():
            full[k, p, rows, :] = own_buf[k, rows, :] + down_buf[k, rows, :]

        @pl.when(stage == stages - 1)
        def _():
            full[k, p, rows, :] = own_buf[k, rows, :] + up_buf[k, rows, :]

        @pl.when(jnp.logical_and(stage > 0, stage < stages - 1))
        def _():
            full[k, p, rows, :] = own_buf[k, rows, :] + up_buf[k, rows, :] + down_buf[k, rows, :]

        for j in range(near):
            peer_copy(h, j).start()

    def forward(h):
        for j in range(near):
            peer_copy(h, j).wait_recv()
            if relayed and j == h % 2:
                peer_copy(h, near).start()

    def forward_far(h):
        for j in range(near, pair_count - 1):
            peer_copy(h, j).wait_recv()

    lower = stage < stages // 2
    ahead, lag = 2, 2

    def early(h):
        @pl.when(lower)
        def _():
            go_up(h)

        @pl.when(jnp.logical_not(lower))
        def _():
            go_down(h)

    def late(h):
        @pl.when(lower)
        def _():
            go_down(h)

        @pl.when(jnp.logical_not(lower))
        def _():
            go_up(h)

    for h in range(count):
        combine(h)
    sorted_count = 0
    for step in range(-ahead, count + 2 * lag):
        if 0 <= step + ahead < count:
            early(step + ahead)
        if 0 <= step < count:
            late(step)
            finish(step)
        if 0 <= step - lag < count:
            forward(step - lag)
        if 0 <= step - 2 * lag < count:
            forward_far(step - 2 * lag)
        if step == 1:
            for j in range(pair_count - 1):
                plane_copy(j).wait_recv()
            plane_keep().wait()
            send_own(0)
        if step == 4:
            send_own(1)
        if step == count - 1:
            send_own(2)
            relay(0)
        if sorted_count < first:
            if sorted_count + slots - 1 < first:
                load_slab(sorted_count + slots - 1)
            finish_slab(sorted_count)
            sorted_count += 1
    while sorted_count < first:
        if sorted_count + slots - 1 < first:
            load_slab(sorted_count + slots - 1)
        finish_slab(sorted_count)
        sorted_count += 1

    blocks = pairs // GROUP
    many = width // both_b
    tile = half_made.shape[-1]

    def main(i, carry):
        @pl.when(i + 3 < steps)
        def _():
            send_own(i + 3)

        @pl.when(i + 1 < steps)
        def _():
            relay(i + 1)

        collect(i)

        @pl.when(i + early_slabs < steps)
        def _():
            slab_copy(i + early_slabs).start()

        late_slab = i + first - steps

        @pl.when(late_slab < steps)
        def _():
            slab_copy(late_slab).wait_recv()
            mate_load(late_slab, 0).start()

        for source in range(stages):
            mate_copy(source, i).wait_recv()
        for s in range(blocks):
            rows = taus[s * GROUP : (s + 1) * GROUP, group(i), :].reshape(spread, -1)
            sorted_taus[s] = jnp.dot(swap[...], rows, preferred_element_type=F32).astype(taus.dtype)
        left = sorted_taus[...].reshape(blocks * spread, -1)

        def part_of(j, inner):
            qs = pl.ds(pl.multiple_of(j * tile, tile), tile)
            for k in range(window):
                right = full[k, :, :, qs].reshape(pair_count * cols, tile)
                made = jnp.dot(left, right, preferred_element_type=F32).astype(half_made.dtype)
                made = made.reshape(blocks, GROUP // many, many * GROUP, tile)
                for u in range(GROUP // many):
                    half_made[u, k] = made[:, u]
            added = acc[...]
            for u in range(GROUP // many):
                right = table[pl.ds(i * GROUP + u * many, many), :, qs].reshape(width, tile)
                added += lax.dot_general(
                    half_made[u].reshape(-1, tile), right, (((1,), (1,)), ((), ())),
                    preferred_element_type=F32,
                )
            acc[...] = added
            return inner

        lax.fori_loop(0, half // tile, part_of, 0)

        @pl.when(late_slab < steps)
        def _():
            mate_load(late_slab, 0).wait()
            sort_slab(late_slab, 0, 1 - core)

        return carry

    lax.fori_loop(0, steps, main, 0)

    for k in range(window):
        for s in range(blocks):
            base = (k * blocks + s) * many * GROUP
            value = acc[base : base + GROUP, 0:both_b]
            for u in range(1, many):
                value += acc[base + u * GROUP : base + (u + 1) * GROUP, u * both_b : (u + 1) * both_b]
            part[s * GROUP : (s + 1) * GROUP, k, :] = value

    def settle_copy(offset):
        there = place(offset)
        spot = pl.ds((there[1] * pair_count + there[0]) * local_pairs, local_pairs)
        return pltpu.make_async_remote_copy(
            src_ref=part.at[spot], dst_ref=inbox.at[t, p],
            send_sem=settle_sems.at[0, offset], recv_sem=settle_sems.at[1, offset],
            device_id=there, device_id_type=MESH,
        )

    for offset in range(1, total):
        settle_copy(offset).start()
    spot = pl.ds((t * pair_count + p) * local_pairs, local_pairs)
    settle_keep = pltpu.make_async_copy(part.at[spot], inbox.at[t, p], local_sems.at[1])
    settle_keep.start()

    for h in range(count):
        core_copy(h).wait_send()

        @pl.when(stage < stages - 1)
        def _():
            up_copy(h).wait_send()

        @pl.when(stage > 0)
        def _():
            down_copy(h).wait_send()

        for j in range(pair_count - 1):
            peer_copy(h, j).wait_send()
    for j in range(pair_count - 1):
        plane_copy(j).wait_send()

    def drain(i, carry):
        slab_copy(i).wait_send()
        for d, shift in enumerate(shifts):
            @pl.when(in_range(shift))
            def _():
                direct_copy(d, i).wait_send()

        for source in range(stages):
            mate_copy(source, i).wait_send()

            @pl.when(jnp.logical_or(goes_up(source), goes_down(source)))
            def _():
                relay_copy(source, i, 1).wait_send()

        return carry

    lax.fori_loop(0, steps, drain, 0)
    settle_keep.wait()
    for offset in range(1, total):
        settle_copy(offset).wait()
    for z in range(stages):
        value = inbox[2 * z, 0]
        for tile_index in (2 * z, 2 * z + 1):
            for source in range(pair_count):
                if tile_index > 2 * z or source:
                    value += inbox[tile_index, source]
        res_ref[:, :, z * both_b : (z + 1) * both_b] = value
    upd_ref[...] = res_ref[...] / den_ref[...]


def ladder(rows, turned, den, factors, pair_count, tile_count):
    window, cols, aux = rows.shape
    half = aux // 2
    own_b, own_d, _ = factors.shape
    local_pairs, virt, _ = turned.shape
    pairs = pair_count * tile_count * local_pairs
    both_b = 2 * own_b
    width = max(256, both_b)
    many = width // both_b
    sub = max(16, cols // 4)
    count = window * cols // sub
    steps = own_d // GROUP
    stages = tile_count // 2
    spread = GROUP * GROUP
    blocks = pairs // GROUP
    tile = min(512, half)
    total = pair_count * tile_count
    kind = rows.dtype
    dma = pltpu.SemaphoreType.DMA
    hbm = pl.BlockSpec(memory_space=pl.ANY)
    piece = pltpu.VMEM((window, cols, half), kind)
    shape = jax.ShapeDtypeStruct((local_pairs, window, virt), F32)
    slots = 3
    return pl.pallas_call(
        functools.partial(ladder_kernel, pair_count, tile_count, sub, width),
        out_shape=(shape, shape, jax.ShapeDtypeStruct((own_b, own_d, half), kind)),
        in_specs=[VMEM, VMEM, VMEM, hbm],
        out_specs=(VMEM, VMEM, pl.BlockSpec(memory_space=pltpu.HBM)),
        scratch_shapes=[pltpu.VMEM((window, pair_count, cols, half), kind)]
        + [piece] * 6
        + [
            pltpu.VMEM((pairs, own_d, virt), kind),
            pltpu.VMEM((blocks, spread, virt), kind),
            pltpu.VMEM((slots, own_b, GROUP, half), kind),
            pltpu.VMEM((own_d, both_b, half), kind),
            pltpu.VMEM((spread, spread), kind),
            pltpu.VMEM((GROUP // many, window, blocks, many * GROUP, tile), kind),
            pltpu.VMEM((window * blocks * many * GROUP, width), F32),
            pltpu.VMEM((pairs, window, both_b), F32),
            pltpu.VMEM((tile_count, pair_count, local_pairs, window, both_b), F32),
            dma((2, count)), dma((2, count)), dma((2, count)), dma((2, pair_count - 1, count)),
            dma((2, pair_count - 1)), dma((4, steps)), dma((stages, steps)), dma((stages, steps)),
            dma((2, stages, steps)), dma((2, steps)), dma((slots,)), dma((2, total)), dma((2,)),
        ],
        compiler_params=pltpu.CompilerParams(
            collective_id=0, has_side_effects=True, vmem_limit_bytes=63 * 1024 * 1024
        ),
    )(rows, turned, den, factors)


def local(amplitudes, factors, pair_list, window_offsets, occupied_energy, virtual_energy):
    pair_count = lax.axis_size("pair")
    tile_count = lax.axis_size("vtile")
    rows, turned, den = prepare(
        amplitudes, factors, pair_list, window_offsets, occupied_energy, virtual_energy
    )
    residual, update, _ = ladder(rows, turned, den, factors, pair_count, tile_count)
    return residual, update


def solution(mesh):
    return jax.shard_map(
        local,
        mesh=mesh,
        in_specs=(
            P(("pair", "vtile"), None, None),
            P("vtile", "pair", None),
            P(("pair", "vtile"), None),
            P(),
            P(),
            P(),
        ),
        out_specs=(P(("pair", "vtile"), None, None), P(("pair", "vtile"), None, None)),
        check_vma=False,
    )
```

```python
import functools

import jax
import jax.numpy as jnp
from jax import lax
from jax.experimental import pallas as pl
from jax.experimental.pallas import tpu as pltpu
from jax.sharding import PartitionSpec as P

MESH = pl.DeviceIdType.MESH
VMEM = pl.BlockSpec(memory_space=pltpu.VMEM)
SMEM = pl.BlockSpec(memory_space=pltpu.SMEM)
F32 = jnp.float32
GROUP = 16


def prepare_kernel(
    offsets_ref, pairs_ref, occupied_ref, energy_ref, virtual_ref, factors_ref, amp_ref,
    rows_ref, turned_ref, den_ref, sems,
):
    t = lax.axis_index("vtile")
    row_count = factors_ref.shape[0]
    window = rows_ref.shape[0]

    def local_row(k):
        return offsets_ref[k] - t * row_count

    def pick(k):
        row = jnp.clip(local_row(k), 0, row_count - 1)
        return pltpu.make_async_copy(factors_ref.at[row], rows_ref.at[k], sems.at[k])

    for k in range(window):
        pick(k).start()
    for pair in range(amp_ref.shape[0]):
        turned_ref[pair] = amp_ref[pair].T
        occupied = occupied_ref[pairs_ref[pair, 0]] + occupied_ref[pairs_ref[pair, 1]]
        for k in range(window):
            den_ref[pair, k : k + 1, :] = (energy_ref[offsets_ref[k]] + virtual_ref[...]) - occupied
    for k in range(window):
        pick(k).wait()
        row = local_row(k)

        @pl.when(jnp.logical_or(row < 0, row >= row_count))
        def _():
            rows_ref[k] = jnp.zeros(rows_ref.shape[1:], rows_ref.dtype)


def prepare(amplitudes, factors, pair_list, window_offsets, occupied_energy, virtual_energy):
    local_pairs, virt, _ = amplitudes.shape
    window = window_offsets.shape[0]
    return pl.pallas_call(
        prepare_kernel,
        out_shape=(
            jax.ShapeDtypeStruct((window,) + factors.shape[1:], factors.dtype),
            jax.ShapeDtypeStruct(amplitudes.shape, amplitudes.dtype),
            jax.ShapeDtypeStruct((local_pairs, window, virt), F32),
        ),
        in_specs=[SMEM, SMEM, SMEM, SMEM, VMEM, pl.BlockSpec(memory_space=pl.ANY), VMEM],
        out_specs=(VMEM, VMEM, VMEM),
        scratch_shapes=[pltpu.SemaphoreType.DMA((window,))],
    )(
        window_offsets, pair_list, occupied_energy, virtual_energy,
        virtual_energy.reshape(1, virt), factors, amplitudes,
    )


def ladder_kernel(
    pair_count, tile_count, sub, width,
    rows_ref, turned_ref, factors_ref,
    res_ref, land_ref,
    full, core_buf, own_buf, up_buf, down_buf, up_out, down_out,
    taus, sorted_taus, stage_buf, table, swap, half_made, acc, part, inbox,
    core_sems, up_sems, down_sems, peer_sems,
    plane_sems, direct_sems, arrive_sems, relay_sems, mate_sems,
    slab_sems, stage_sems, settle_sems, local_sems,
):
    p = lax.axis_index("pair")
    t = lax.axis_index("vtile")
    core = lax.rem(t, 2)
    stage = t // 2
    stages = tile_count // 2
    total = pair_count * tile_count
    me = p * tile_count + t
    window, cols, aux = rows_ref.shape
    half = aux // 2
    own_b, own_d, _ = factors_ref.shape
    both_b = 2 * own_b
    local_pairs = turned_ref.shape[0]
    block = pair_count * local_pairs
    pairs = tile_count * block
    steps = own_d // GROUP
    spread = swap.shape[0]
    mate = (p, stage * 2 + (1 - core))
    above = (p, t + 2)
    below = (p, t - 2)
    relayed = pair_count == 4
    if relayed:
        across = p + 1 - 2 * lax.rem(p, 2)
        along = lax.rem(p + 2, 4)
        sources = [across, along, lax.rem(across + 2, 4)]
        peers = [(source, t) for source in sources]
    else:
        peers = [(lax.rem(p + j, pair_count), t) for j in range(1, pair_count)]
        sources = [lax.rem(p + pair_count - j, pair_count) for j in range(1, pair_count)]
    near = 2 if relayed else pair_count - 1

    def place(offset):
        other = lax.rem(me + offset, total)
        return other // tile_count, lax.rem(other, tile_count)

    barrier = pltpu.get_barrier_semaphore()
    shifts = [shift for shift in (-2, -1, 1, 2) if abs(shift) < stages]

    def in_range(shift):
        return jnp.logical_and(stage + shift >= 0, stage + shift < stages)

    for device in [mate] + peers:
        pl.semaphore_signal(barrier, inc=1, device_id=device, device_id_type=MESH)
    expected = pair_count
    for shift in shifts:
        @pl.when(in_range(shift))
        def _():
            pl.semaphore_signal(
                barrier, inc=1, device_id=(p, t + 2 * shift), device_id_type=MESH
            )

        expected += in_range(shift).astype(jnp.int32)
    pl.semaphore_wait(barrier, expected)

    mine_lanes = pl.ds(pl.multiple_of(core * half, half), half)
    mate_lanes = pl.ds(pl.multiple_of((1 - core) * half, half), half)
    chunks = [(k, pl.ds(s * sub, sub)) for k in range(window) for s in range(cols // sub)]
    count = len(chunks)

    def remote(src, dst, sems, index, device):
        return pltpu.make_async_remote_copy(
            src_ref=src, dst_ref=dst, send_sem=sems.at[(0,) + index], recv_sem=sems.at[(1,) + index],
            device_id=device, device_id_type=MESH,
        )

    def group(i):
        return pl.ds(pl.multiple_of(i * GROUP, GROUP), GROUP)

    def core_copy(h):
        k, rows = chunks[h]
        return remote(rows_ref.at[k, rows, mate_lanes], core_buf.at[k, rows], core_sems, (h,), mate)

    def up_copy(h):
        k, rows = chunks[h]
        return remote(up_out.at[k, rows], up_buf.at[k, rows], up_sems, (h,), above)

    def down_copy(h):
        k, rows = chunks[h]
        return remote(down_out.at[k, rows], down_buf.at[k, rows], down_sems, (h,), below)

    def peer_copy(h, j):
        k, rows = chunks[h]
        if j >= near:
            spot = full.at[k, sources[h % 2], rows]
            return remote(spot, spot, peer_sems, (j, h), peers[1 - h % 2])
        spot = full.at[k, p, rows]
        return remote(spot, spot, peer_sems, (j, h), peers[j])

    def plane_copy(j):
        rows = pl.ds(pl.multiple_of(peers[j][0] * own_d, own_d), own_d)
        spot = taus.at[pl.ds((t * pair_count + p) * local_pairs, local_pairs)]
        return remote(turned_ref.at[:, rows], spot, plane_sems, (j,), peers[j])

    def plane_keep():
        rows = pl.ds(pl.multiple_of(p * own_d, own_d), own_d)
        spot = taus.at[pl.ds((t * pair_count + p) * local_pairs, local_pairs)]
        return pltpu.make_async_copy(turned_ref.at[:, rows], spot, local_sems.at[0])

    def tau_spot(tile, i):
        return taus.at[pl.ds(tile * block, block), group(i)]

    def direct_copy(d, i):
        return pltpu.make_async_remote_copy(
            src_ref=tau_spot(t, i), dst_ref=tau_spot(t, i),
            send_sem=direct_sems.at[d, i], recv_sem=arrive_sems.at[stage, i],
            device_id=(p, t + 2 * shifts[d]), device_id_type=MESH,
        )

    def relay_copy(source, i, shift):
        spot = tau_spot(2 * source + core, i)
        return pltpu.make_async_remote_copy(
            src_ref=spot, dst_ref=spot,
            send_sem=relay_sems.at[source, i], recv_sem=arrive_sems.at[source, i],
            device_id=(p, t + 2 * shift), device_id_type=MESH,
        )

    def mate_copy(source, i):
        spot = tau_spot(2 * source + core, i)
        return remote(spot, spot, mate_sems, (source, i), mate)

    def goes_up(source):
        return jnp.logical_and(stage >= source + 2, stage + 1 < stages)

    def goes_down(source):
        return jnp.logical_and(stage <= source - 2, stage >= 1)

    def send_own(i):
        for d, shift in enumerate(shifts):
            @pl.when(in_range(shift))
            def _():
                direct_copy(d, i).start()

    def relay(i):
        for source in range(stages):
            @pl.when(goes_up(source))
            def _():
                relay_copy(source, i, 1).wait_recv()
                relay_copy(source, i, 1).start()

            @pl.when(goes_down(source))
            def _():
                relay_copy(source, i, -1).wait_recv()
                relay_copy(source, i, -1).start()

    def collect(i):
        for source in range(stages):
            passed = jnp.logical_or(goes_up(source), goes_down(source))

            @pl.when(jnp.logical_not(jnp.logical_or(passed, stage == source)))
            def _():
                relay_copy(source, i, 1).wait_recv()

            mate_copy(source, i).start()

    def slab_copy(i):
        return remote(
            factors_ref.at[:, group(i), mate_lanes], land_ref.at[:, group(i)], slab_sems, (i,), mate
        )

    slots = stage_buf.shape[0]

    def own_load(i, slot):
        return pltpu.make_async_copy(
            factors_ref.at[:, group(i), mine_lanes], stage_buf.at[slot], stage_sems.at[slot]
        )

    def mate_load(i, slot):
        return pltpu.make_async_copy(land_ref.at[:, group(i)], stage_buf.at[slot], stage_sems.at[slot])

    def sort_slab(i, slot, side):
        def one(b, carry):
            rows = stage_buf[slot, group(b)].reshape(GROUP * GROUP, half)
            made = jnp.dot(swap[...], rows, preferred_element_type=F32).astype(table.dtype)
            spot = pl.ds(pl.multiple_of(side * own_b + b * GROUP, GROUP), GROUP)
            table[group(i), spot, :] = made.reshape(GROUP, GROUP, half)
            return carry

        lax.fori_loop(0, own_b // GROUP, one, 0)

    def load_slab(n):
        if n < steps:
            own_load(n, n % slots).start()
        else:
            slab_copy(n - steps).wait_recv()
            mate_load(n - steps, n % slots).start()

    def finish_slab(n):
        if n < steps:
            own_load(n, n % slots).wait()
            sort_slab(n, n % slots, core)
        else:
            mate_load(n - steps, n % slots).wait()
            sort_slab(n - steps, n % slots, 1 - core)

    slabs = 2 * steps
    own_steps = dict(zip((0, 2, 4, 6, 9), range(steps)))
    relay_steps = dict(zip((3, 5, 7, 10), range(steps)))

    for h in range(count):
        core_copy(h).start()
    for j in range(pair_count - 1):
        plane_copy(j).start()
    plane_keep().start()
    for i in range(steps):
        slab_copy(i).start()
    for n in range(slots - 1):
        load_slab(n)
    lanes = lax.broadcasted_iota(jnp.int32, (spread, spread), 1)
    lines = lax.broadcasted_iota(jnp.int32, (spread, spread), 0)
    swap[...] = jnp.where(
        jnp.logical_and(lines // GROUP == lanes % GROUP, lines % GROUP == lanes // GROUP), 1.0, 0.0
    ).astype(swap.dtype)
    acc[...] = jnp.zeros_like(acc)

    def combine(h):
        k, rows = chunks[h]
        core_copy(h).wait_recv()
        own_buf[k, rows, :] = rows_ref[k, rows, mine_lanes] + core_buf[k, rows, :]

        @pl.when(stage == 0)
        def _():
            up_out[k, rows, :] = own_buf[k, rows, :]
            up_copy(h).start()

        @pl.when(stage == stages - 1)
        def _():
            down_out[k, rows, :] = own_buf[k, rows, :]
            down_copy(h).start()

    def go_up(h):
        k, rows = chunks[h]

        @pl.when(stage > 0)
        def _():
            up_copy(h).wait_recv()

            @pl.when(stage < stages - 1)
            def _():
                up_out[k, rows, :] = own_buf[k, rows, :] + up_buf[k, rows, :]
                up_copy(h).start()

    def go_down(h):
        k, rows = chunks[h]

        @pl.when(stage < stages - 1)
        def _():
            down_copy(h).wait_recv()

            @pl.when(stage > 0)
            def _():
                down_out[k, rows, :] = own_buf[k, rows, :] + down_buf[k, rows, :]
                down_copy(h).start()

    def finish(h):
        k, rows = chunks[h]

        @pl.when(stage == 0)
        def _():
            full[k, p, rows, :] = own_buf[k, rows, :] + down_buf[k, rows, :]

        @pl.when(stage == stages - 1)
        def _():
            full[k, p, rows, :] = own_buf[k, rows, :] + up_buf[k, rows, :]

        @pl.when(jnp.logical_and(stage > 0, stage < stages - 1))
        def _():
            full[k, p, rows, :] = own_buf[k, rows, :] + up_buf[k, rows, :] + down_buf[k, rows, :]

        for j in range(near):
            peer_copy(h, j).start()

    def forward(h):
        for j in range(near):
            peer_copy(h, j).wait_recv()
            if relayed and j == h % 2:
                peer_copy(h, near).start()

    def forward_far(h):
        for j in range(near, pair_count - 1):
            peer_copy(h, j).wait_recv()

    lower = stage < stages // 2
    ahead, lag = 2, 2

    def early(h):
        @pl.when(lower)
        def _():
            go_up(h)

        @pl.when(jnp.logical_not(lower))
        def _():
            go_down(h)

    def late(h):
        @pl.when(lower)
        def _():
            go_down(h)

        @pl.when(jnp.logical_not(lower))
        def _():
            go_up(h)

    for h in range(count):
        combine(h)
    sorted_count = 0
    for step in range(-ahead, count + 2 * lag):
        if 0 <= step + ahead < count:
            early(step + ahead)
        if 0 <= step < count:
            late(step)
            finish(step)
        if 0 <= step - lag < count:
            forward(step - lag)
        if 0 <= step - 2 * lag < count:
            forward_far(step - 2 * lag)
        if step == 0:
            for j in range(pair_count - 1):
                plane_copy(j).wait_recv()
            plane_keep().wait()
        if step in own_steps:
            send_own(own_steps[step])
        if step in relay_steps:
            relay(relay_steps[step])
        if sorted_count < slabs:
            if sorted_count + slots - 1 < slabs:
                load_slab(sorted_count + slots - 1)
            finish_slab(sorted_count)
            sorted_count += 1
    while sorted_count < slabs:
        if sorted_count + slots - 1 < slabs:
            load_slab(sorted_count + slots - 1)
        finish_slab(sorted_count)
        sorted_count += 1
    collect(0)

    blocks = pairs // GROUP
    many = width // both_b
    tile = half_made.shape[-1]

    def main(i, carry):
        @pl.when(i + len(own_steps) < steps)
        def _():
            send_own(i + len(own_steps))

        for source in range(stages):
            mate_copy(source, i).wait_recv()

        @pl.when(jnp.logical_and(i + 2 >= len(relay_steps), i + 2 < steps))
        def _():
            relay(i + 2)

        @pl.when(i + 1 < steps)
        def _():
            collect(i + 1)

        for s in range(blocks):
            rows = taus[s * GROUP : (s + 1) * GROUP, group(i), :].reshape(spread, -1)
            sorted_taus[s] = jnp.dot(swap[...], rows, preferred_element_type=F32).astype(taus.dtype)
        left = sorted_taus[...].reshape(blocks * spread, -1)

        def part_of(j, inner):
            qs = pl.ds(pl.multiple_of(j * tile, tile), tile)
            for k in range(window):
                right = full[k, :, :, qs].reshape(pair_count * cols, tile)
                made = jnp.dot(left, right, preferred_element_type=F32).astype(half_made.dtype)
                made = made.reshape(blocks, GROUP // many, many * GROUP, tile)
                for u in range(GROUP // many):
                    half_made[u, k] = made[:, u]
            added = acc[...]
            for u in range(GROUP // many):
                right = table[pl.ds(i * GROUP + u * many, many), :, qs].reshape(width, tile)
                added += lax.dot_general(
                    half_made[u].reshape(-1, tile), right, (((1,), (1,)), ((), ())),
                    preferred_element_type=F32,
                )
            acc[...] = added
            return inner

        lax.fori_loop(0, half // tile, part_of, 0)

        return carry

    lax.fori_loop(0, steps, main, 0)

    for k in range(window):
        for s in range(blocks):
            base = (k * blocks + s) * many * GROUP
            value = acc[base : base + GROUP, 0:both_b]
            for u in range(1, many):
                value += acc[base + u * GROUP : base + (u + 1) * GROUP, u * both_b : (u + 1) * both_b]
            part[s * GROUP : (s + 1) * GROUP, k, :] = value

    def settle_copy(offset):
        there = place(offset)
        spot = pl.ds((there[1] * pair_count + there[0]) * local_pairs, local_pairs)
        return pltpu.make_async_remote_copy(
            src_ref=part.at[spot], dst_ref=inbox.at[t, p],
            send_sem=settle_sems.at[0, offset], recv_sem=settle_sems.at[1, offset],
            device_id=there, device_id_type=MESH,
        )

    for offset in range(1, total):
        settle_copy(offset).start()
    spot = pl.ds((t * pair_count + p) * local_pairs, local_pairs)
    settle_keep = pltpu.make_async_copy(part.at[spot], inbox.at[t, p], local_sems.at[1])
    settle_keep.start()

    for h in range(count):
        core_copy(h).wait_send()

        @pl.when(stage < stages - 1)
        def _():
            up_copy(h).wait_send()

        @pl.when(stage > 0)
        def _():
            down_copy(h).wait_send()

        for j in range(pair_count - 1):
            peer_copy(h, j).wait_send()
    for j in range(pair_count - 1):
        plane_copy(j).wait_send()

    def drain(i, carry):
        slab_copy(i).wait_send()
        for d, shift in enumerate(shifts):
            @pl.when(in_range(shift))
            def _():
                direct_copy(d, i).wait_send()

        for source in range(stages):
            mate_copy(source, i).wait_send()

            @pl.when(jnp.logical_or(goes_up(source), goes_down(source)))
            def _():
                relay_copy(source, i, 1).wait_send()

        return carry

    lax.fori_loop(0, steps, drain, 0)
    settle_keep.wait()
    for offset in range(1, total):
        settle_copy(offset).wait()
    for z in range(stages):
        value = inbox[2 * z, 0]
        for tile_index in (2 * z, 2 * z + 1):
            for source in range(pair_count):
                if tile_index > 2 * z or source:
                    value += inbox[tile_index, source]
        res_ref[:, :, z * both_b : (z + 1) * both_b] = value


def settle_kernel(sum_ref, den_ref, res_ref, upd_ref):
    res_ref[...] = sum_ref[...]
    upd_ref[...] = sum_ref[...] / den_ref[...]


def settle(sums, den):
    shape = jax.ShapeDtypeStruct(sums.shape, F32)
    return pl.pallas_call(
        settle_kernel, out_shape=(shape, shape), in_specs=[VMEM, VMEM], out_specs=(VMEM, VMEM)
    )(sums, den)


def ladder(rows, turned, factors, pair_count, tile_count):
    window, cols, aux = rows.shape
    half = aux // 2
    own_b, own_d, _ = factors.shape
    local_pairs, virt, _ = turned.shape
    pairs = pair_count * tile_count * local_pairs
    both_b = 2 * own_b
    width = max(512, both_b)
    many = width // both_b
    sub = max(16, cols // 4)
    count = window * cols // sub
    steps = own_d // GROUP
    stages = tile_count // 2
    spread = GROUP * GROUP
    blocks = pairs // GROUP
    tile = min(512, half)
    total = pair_count * tile_count
    kind = rows.dtype
    dma = pltpu.SemaphoreType.DMA
    hbm = pl.BlockSpec(memory_space=pl.ANY)
    piece = pltpu.VMEM((window, cols, half), kind)
    shape = jax.ShapeDtypeStruct((local_pairs, window, virt), F32)
    slots = 3
    return pl.pallas_call(
        functools.partial(ladder_kernel, pair_count, tile_count, sub, width),
        out_shape=(shape, jax.ShapeDtypeStruct((own_b, own_d, half), kind)),
        in_specs=[VMEM, VMEM, hbm],
        out_specs=(VMEM, pl.BlockSpec(memory_space=pltpu.HBM)),
        scratch_shapes=[pltpu.VMEM((window, pair_count, cols, half), kind)]
        + [piece] * 6
        + [
            pltpu.VMEM((pairs, own_d, virt), kind),
            pltpu.VMEM((blocks, spread, virt), kind),
            pltpu.VMEM((slots, own_b, GROUP, half), kind),
            pltpu.VMEM((own_d, both_b, half), kind),
            pltpu.VMEM((spread, spread), kind),
            pltpu.VMEM((GROUP // many, window, blocks, many * GROUP, tile), kind),
            pltpu.VMEM((window * blocks * many * GROUP, width), F32),
            pltpu.VMEM((pairs, window, both_b), F32),
            pltpu.VMEM((tile_count, pair_count, local_pairs, window, both_b), F32),
            dma((2, count)), dma((2, count)), dma((2, count)), dma((2, pair_count - 1, count)),
            dma((2, pair_count - 1)), dma((4, steps)), dma((stages, steps)), dma((stages, steps)),
            dma((2, stages, steps)), dma((2, steps)), dma((slots,)), dma((2, total)), dma((2,)),
        ],
        compiler_params=pltpu.CompilerParams(
            collective_id=0, has_side_effects=True, vmem_limit_bytes=63 * 1024 * 1024
        ),
    )(rows, turned, factors)


def local(amplitudes, factors, pair_list, window_offsets, occupied_energy, virtual_energy):
    pair_count = lax.axis_size("pair")
    tile_count = lax.axis_size("vtile")
    rows, turned, den = prepare(
        amplitudes, factors, pair_list, window_offsets, occupied_energy, virtual_energy
    )
    sums, _ = ladder(rows, turned, factors, pair_count, tile_count)
    return settle(sums, den)


def solution(mesh):
    return jax.shard_map(
        local,
        mesh=mesh,
        in_specs=(
            P(("pair", "vtile"), None, None),
            P("vtile", "pair", None),
            P(("pair", "vtile"), None),
            P(),
            P(),
            P(),
        ),
        out_specs=(P(("pair", "vtile"), None, None), P(("pair", "vtile"), None, None)),
        check_vma=False,
    )
```

```python
import functools

import jax
import jax.numpy as jnp
from jax import lax
from jax.experimental import pallas as pl
from jax.experimental.pallas import tpu as pltpu
from jax.sharding import PartitionSpec as P

MESH = pl.DeviceIdType.MESH
VMEM = pl.BlockSpec(memory_space=pltpu.VMEM)
SMEM = pl.BlockSpec(memory_space=pltpu.SMEM)
HBM = pl.BlockSpec(memory_space=pltpu.HBM)
F32 = jnp.float32
GROUP = 16
OWN_STEPS = (4, 6, 7, 8, 9, 10, 11)
RELAY_STEPS = (8, 10, 11)


def prepare_kernel(
    offsets_ref, pairs_ref, occupied_ref, energy_ref, virtual_ref, factors_ref, amp_ref,
    rows_ref, turned_ref, den_ref, sems,
):
    t = lax.axis_index("vtile")
    row_count = factors_ref.shape[0]
    window = rows_ref.shape[0]

    def local_row(k):
        return offsets_ref[k] - t * row_count

    def pick(k):
        row = jnp.clip(local_row(k), 0, row_count - 1)
        return pltpu.make_async_copy(factors_ref.at[row], rows_ref.at[k], sems.at[k])

    for k in range(window):
        pick(k).start()
    for pair in range(amp_ref.shape[0]):
        turned_ref[pair] = amp_ref[pair].T
        occupied = occupied_ref[pairs_ref[pair, 0]] + occupied_ref[pairs_ref[pair, 1]]
        for k in range(window):
            den_ref[pair, k : k + 1, :] = (energy_ref[offsets_ref[k]] + virtual_ref[...]) - occupied
    for k in range(window):
        pick(k).wait()
        row = local_row(k)

        @pl.when(jnp.logical_or(row < 0, row >= row_count))
        def _():
            rows_ref[k] = jnp.zeros(rows_ref.shape[1:], rows_ref.dtype)


def prepare(amplitudes, factors, pair_list, window_offsets, occupied_energy, virtual_energy):
    local_pairs, virt, _ = amplitudes.shape
    window = window_offsets.shape[0]
    return pl.pallas_call(
        prepare_kernel,
        out_shape=(
            jax.ShapeDtypeStruct((window,) + factors.shape[1:], factors.dtype),
            jax.ShapeDtypeStruct(amplitudes.shape, amplitudes.dtype),
            jax.ShapeDtypeStruct((local_pairs, window, virt), F32),
        ),
        in_specs=[SMEM, SMEM, SMEM, SMEM, VMEM, HBM, VMEM],
        out_specs=(VMEM, VMEM, VMEM),
        scratch_shapes=[pltpu.SemaphoreType.DMA((window,))],
    )(
        window_offsets, pair_list, occupied_energy, virtual_energy,
        virtual_energy.reshape(1, virt), factors, amplitudes,
    )


def ladder_kernel(
    pair_count, tile_count, sub, width,
    rows_ref, turned_ref, factors_ref,
    res_ref,
    full, core_buf, own_buf, up_buf, down_buf, up_out, down_out,
    taus, sorted_taus, table, swap, half_made, acc, part, inbox,
    sent_sems, core_sems, up_sems, down_sems, peer_sems,
    plane_sems, direct_sems, arrive_sems, relay_sems, mate_sent, mate_sems,
    slab_sent, slab_sems, load_sems, settle_sems, local_sems,
):
    p = lax.axis_index("pair")
    t = lax.axis_index("vtile")
    core = lax.rem(t, 2)
    stage = t // 2
    stages = tile_count // 2
    total = pair_count * tile_count
    me = p * tile_count + t
    window, cols, aux = rows_ref.shape
    half = aux // 2
    own_b, own_d, _ = factors_ref.shape
    both_b = 2 * own_b
    local_pairs = turned_ref.shape[0]
    block = pair_count * local_pairs
    pairs = tile_count * block
    steps = own_d // GROUP
    spread = swap.shape[0]
    mate = (p, stage * 2 + (1 - core))
    above = (p, t + 2)
    below = (p, t - 2)
    relayed = pair_count == 4
    if relayed:
        across = p + 1 - 2 * lax.rem(p, 2)
        along = lax.rem(p + 2, 4)
        sources = [across, along, lax.rem(across + 2, 4)]
        peers = [(source, t) for source in sources]
    else:
        peers = [(lax.rem(p + j, pair_count), t) for j in range(1, pair_count)]
        sources = [lax.rem(p + pair_count - j, pair_count) for j in range(1, pair_count)]
    near = 2 if relayed else pair_count - 1

    def place(offset):
        other = lax.rem(me + offset, total)
        return other // tile_count, lax.rem(other, tile_count)

    barrier = pltpu.get_barrier_semaphore()
    shifts = [shift for shift in (-2, -1, 1, 2) if abs(shift) < stages]

    def in_range(shift):
        return jnp.logical_and(stage + shift >= 0, stage + shift < stages)

    for device in [mate] + peers:
        pl.semaphore_signal(barrier, inc=1, device_id=device, device_id_type=MESH)
    expected = pair_count
    for shift in shifts:
        @pl.when(in_range(shift))
        def _():
            pl.semaphore_signal(
                barrier, inc=1, device_id=(p, t + 2 * shift), device_id_type=MESH
            )

        expected += in_range(shift).astype(jnp.int32)
    pl.semaphore_wait(barrier, expected)

    mine_lanes = pl.ds(pl.multiple_of(core * half, half), half)
    mate_lanes = pl.ds(pl.multiple_of((1 - core) * half, half), half)
    chunks = [(k, pl.ds(s * sub, sub)) for k in range(window) for s in range(cols // sub)]
    count = len(chunks)

    def remote(src, dst, sems, index, device):
        return pltpu.make_async_remote_copy(
            src_ref=src, dst_ref=dst, send_sem=sems[0], recv_sem=sems[1].at[index],
            device_id=device, device_id_type=MESH,
        )

    def all_sent(ref, sem):
        pltpu.make_async_remote_copy(
            src_ref=ref, dst_ref=ref, send_sem=sem, recv_sem=sem,
            device_id=mate, device_id_type=MESH,
        ).wait_recv()

    def group(i):
        return pl.ds(pl.multiple_of(i * GROUP, GROUP), GROUP)

    def core_copy(h):
        k, rows = chunks[h]
        return remote(rows_ref.at[k, rows, mate_lanes], core_buf.at[k, rows], (sent_sems.at[0], core_sems), (h,), mate)

    def up_copy(h):
        k, rows = chunks[h]
        return remote(up_out.at[k, rows], up_buf.at[k, rows], (sent_sems.at[1], up_sems), (h,), above)

    def down_copy(h):
        k, rows = chunks[h]
        return remote(down_out.at[k, rows], down_buf.at[k, rows], (sent_sems.at[2], down_sems), (h,), below)

    def peer_copy(h, j):
        k, rows = chunks[h]
        if j >= near:
            spot = full.at[k, sources[h % 2], rows]
            return remote(spot, spot, (sent_sems.at[4 + j], peer_sems), (j, h), peers[1 - h % 2])
        spot = full.at[k, p, rows]
        return remote(spot, spot, (sent_sems.at[4 + j], peer_sems), (j, h), peers[j])

    def plane_copy(j):
        there = peers[j][0]
        rows = pl.ds(pl.multiple_of(there * own_d, own_d), own_d)
        turn = lax.rem(p - there + pair_count, pair_count)
        spot = taus.at[pl.ds((t * pair_count + turn) * local_pairs, local_pairs)]
        return remote(turned_ref.at[:, rows], spot, (sent_sems.at[3], plane_sems), (0,), peers[j])

    def plane_keep():
        rows = pl.ds(pl.multiple_of(p * own_d, own_d), own_d)
        spot = taus.at[pl.ds(t * block, local_pairs)]
        return pltpu.make_async_copy(turned_ref.at[:, rows], spot, local_sems.at[0])

    def tau_spot(tile, i):
        return taus.at[pl.ds(tile * block, block), group(i)]

    def direct_copy(d, i):
        return pltpu.make_async_remote_copy(
            src_ref=tau_spot(t, i), dst_ref=tau_spot(t, i),
            send_sem=direct_sems.at[d], recv_sem=arrive_sems.at[stage, i],
            device_id=(p, t + 2 * shifts[d]), device_id_type=MESH,
        )

    def relay_copy(source, i, shift):
        spot = tau_spot(2 * source + core, i)
        return pltpu.make_async_remote_copy(
            src_ref=spot, dst_ref=spot,
            send_sem=relay_sems.at[source], recv_sem=arrive_sems.at[source, i],
            device_id=(p, t + 2 * shift), device_id_type=MESH,
        )

    def mate_copy(source, i):
        spot = tau_spot(2 * source + core, i)
        return remote(spot, spot, (mate_sent.at[source], mate_sems), (i,), mate)

    def goes_up(source):
        return jnp.logical_and(stage >= source + 2, stage + 1 < stages)

    def goes_down(source):
        return jnp.logical_and(stage <= source - 2, stage >= 1)

    def mate_wait(i):
        all_sent(taus.at[pl.ds(0, stages * block), group(i)], mate_sems.at[i])

    def send_own(i):
        for d, shift in enumerate(shifts):
            @pl.when(in_range(shift))
            def _():
                direct_copy(d, i).start()

    def relay(i):
        for source in range(stages):
            @pl.when(goes_up(source))
            def _():
                relay_copy(source, i, 1).wait_recv()
                relay_copy(source, i, 1).start()

            @pl.when(goes_down(source))
            def _():
                relay_copy(source, i, -1).wait_recv()
                relay_copy(source, i, -1).start()

    def collect(i):
        for source in range(stages):
            passed = jnp.logical_or(goes_up(source), goes_down(source))

            @pl.when(jnp.logical_not(jnp.logical_or(passed, stage == source)))
            def _():
                relay_copy(source, i, 1).wait_recv()

            mate_copy(source, i).start()

    def mate_slab(i):
        return remote(factors_ref.at[:, group(i), mate_lanes], table.at[core, i], (slab_sent.at[i], slab_sems), (i,), mate)

    def own_slab(i):
        return pltpu.make_async_copy(
            factors_ref.at[:, group(i), mine_lanes], table.at[core, i], load_sems.at[i]
        )

    def sort_slab(side, i):
        def one(b, carry):
            rows = table[side, i, group(b)].reshape(spread, half)
            made = jnp.dot(swap[...], rows, preferred_element_type=F32).astype(table.dtype)
            table[side, i, group(b)] = made.reshape(GROUP, GROUP, half)
            return carry

        lax.fori_loop(0, own_b // GROUP, one, 0)

    def finish_slab(n):
        if n < steps:
            own_slab(n).wait()
            sort_slab(core, n)
        else:
            mate_slab(n - steps).wait_recv()
            sort_slab(1 - core, n - steps)

    slabs = 2 * steps
    own_steps = dict(zip(OWN_STEPS, range(steps)))
    relay_steps = dict(zip(RELAY_STEPS, range(steps)))
    relays = len(relay_steps)
    sends = len(own_steps)

    for h in range(count):
        core_copy(h).start()
    for j in range(pair_count - 1):
        plane_copy(j).start()
    plane_keep().start()
    for i in range(steps):
        own_slab(i).start()
        mate_slab(i).start()
    lanes = lax.broadcasted_iota(jnp.int32, (spread, spread), 1)
    lines = lax.broadcasted_iota(jnp.int32, (spread, spread), 0)
    swap[...] = jnp.where(
        jnp.logical_and(lines // GROUP == lanes % GROUP, lines % GROUP == lanes // GROUP), 1.0, 0.0
    ).astype(swap.dtype)
    acc[...] = jnp.zeros_like(acc)

    def combine(h):
        k, rows = chunks[h]
        core_copy(h).wait_recv()
        own_buf[k, rows, :] = rows_ref[k, rows, mine_lanes] + core_buf[k, rows, :]

        @pl.when(stage == 0)
        def _():
            up_out[k, rows, :] = own_buf[k, rows, :]
            up_copy(h).start()

        @pl.when(stage == stages - 1)
        def _():
            down_out[k, rows, :] = own_buf[k, rows, :]
            down_copy(h).start()

    def go_up(h):
        k, rows = chunks[h]

        @pl.when(stage > 0)
        def _():
            up_copy(h).wait_recv()

            @pl.when(stage < stages - 1)
            def _():
                up_out[k, rows, :] = own_buf[k, rows, :] + up_buf[k, rows, :]
                up_copy(h).start()

    def go_down(h):
        k, rows = chunks[h]

        @pl.when(stage < stages - 1)
        def _():
            down_copy(h).wait_recv()

            @pl.when(stage > 0)
            def _():
                down_out[k, rows, :] = own_buf[k, rows, :] + down_buf[k, rows, :]
                down_copy(h).start()

    def finish(h):
        k, rows = chunks[h]

        @pl.when(stage == 0)
        def _():
            full[k, p, rows, :] = own_buf[k, rows, :] + down_buf[k, rows, :]

        @pl.when(stage == stages - 1)
        def _():
            full[k, p, rows, :] = own_buf[k, rows, :] + up_buf[k, rows, :]

        @pl.when(jnp.logical_and(stage > 0, stage < stages - 1))
        def _():
            full[k, p, rows, :] = own_buf[k, rows, :] + up_buf[k, rows, :] + down_buf[k, rows, :]

        for j in range(near):
            peer_copy(h, j).start()

    def forward(h):
        for j in range(near):
            peer_copy(h, j).wait_recv()
            if relayed and j == h % 2:
                peer_copy(h, near).start()

    def forward_far(h):
        for j in range(near, pair_count - 1):
            peer_copy(h, j).wait_recv()

    lower = stage < stages // 2
    ahead, lag = 2, 2

    def early(h):
        @pl.when(lower)
        def _():
            go_up(h)

        @pl.when(jnp.logical_not(lower))
        def _():
            go_down(h)

    def late(h):
        @pl.when(lower)
        def _():
            go_down(h)

        @pl.when(jnp.logical_not(lower))
        def _():
            go_up(h)

    for h in range(count):
        combine(h)
    sorted_count = 0
    for step in range(-ahead, count + 2 * lag):
        if 0 <= step + ahead < count:
            early(step + ahead)
        if 0 <= step < count:
            late(step)
            finish(step)
        if 0 <= step - lag < count:
            forward(step - lag)
        if 0 <= step - 2 * lag < count:
            forward_far(step - 2 * lag)
        if step == 0:
            all_sent(taus.at[pl.ds(t * block + local_pairs, block - local_pairs)], plane_sems.at[0])
            plane_keep().wait()
        if step in own_steps:
            send_own(own_steps[step])
        if step in relay_steps:
            relay(relay_steps[step])
        if sorted_count < slabs:
            finish_slab(sorted_count)
            sorted_count += 1
    while sorted_count < slabs:
        finish_slab(sorted_count)
        sorted_count += 1
    for i in range(relays, min(2, steps)):
        relay(i)
    collect(0)

    blocks = pairs // GROUP
    many = width // both_b
    tile = half_made.shape[-1]

    def main(i, carry):
        @pl.when(i + sends < steps)
        def _():
            send_own(i + sends)

        mate_wait(i)

        @pl.when(jnp.logical_and(i + 2 >= relays, i + 2 < steps))
        def _():
            relay(i + 2)

        @pl.when(i + 1 < steps)
        def _():
            collect(i + 1)

        for s in range(blocks):
            rows = taus[s * GROUP : (s + 1) * GROUP, group(i), :].reshape(spread, -1)
            sorted_taus[s] = jnp.dot(swap[...], rows, preferred_element_type=F32).astype(taus.dtype)
        left = sorted_taus[...].reshape(blocks * spread, -1)

        def part_of(j, inner):
            qs = pl.ds(pl.multiple_of(j * tile, tile), tile)
            for k in range(window):
                right = full[k, :, :, qs].reshape(pair_count * cols, tile)
                made = jnp.dot(left, right, preferred_element_type=F32).astype(half_made.dtype)
                made = made.reshape(blocks, GROUP // many, many * GROUP, tile)
                for u in range(GROUP // many):
                    half_made[u, k] = made[:, u]
            added = acc[...]
            for u in range(GROUP // many):
                right = jnp.concatenate(
                    [
                        table[side, i, b + u * many : b + (u + 1) * many, :, qs].reshape(-1, tile)
                        for side in range(2)
                        for b in range(0, own_b, GROUP)
                    ]
                )
                added += lax.dot_general(
                    half_made[u].reshape(-1, tile), right, (((1,), (1,)), ((), ())),
                    preferred_element_type=F32,
                )
            acc[...] = added
            return inner

        lax.fori_loop(0, half // tile, part_of, 0)

        return carry

    lax.fori_loop(0, steps, main, 0)

    lines = lax.broadcasted_iota(jnp.int32, (width, both_b), 0)
    lanes = lax.broadcasted_iota(jnp.int32, (width, both_b), 1)
    same_block = lines // (many * GROUP) == lanes // GROUP
    choose = jnp.where(jnp.logical_and(same_block, lines % GROUP == lanes % GROUP), 1.0, 0.0)
    which = lax.broadcasted_iota(jnp.int32, (GROUP, width), 1) // GROUP % many
    for k in range(window):
        for s in range(blocks):
            base = (k * blocks + s) * many * GROUP
            value = jnp.where(which == 0, acc[base : base + GROUP, :], 0.0)
            for u in range(1, many):
                rows = acc[base + u * GROUP : base + (u + 1) * GROUP, :]
                value += jnp.where(which == u, rows, 0.0)
            part[s * GROUP : (s + 1) * GROUP, k, :] = jnp.dot(
                value, choose, precision=lax.Precision.HIGHEST, preferred_element_type=F32
            )

    def settle_copy(offset):
        there = place(offset)
        turn = lax.rem(there[0] - p + pair_count, pair_count)
        spot = pl.ds((there[1] * pair_count + turn) * local_pairs, local_pairs)
        return pltpu.make_async_remote_copy(
            src_ref=part.at[spot], dst_ref=inbox.at[t, p],
            send_sem=settle_sems.at[0], recv_sem=settle_sems.at[1],
            device_id=there, device_id_type=MESH,
        )

    for offset in range(1, total):
        settle_copy(offset).start()
    spot = pl.ds(t * block, local_pairs)
    settle_keep = pltpu.make_async_copy(part.at[spot], inbox.at[t, p], local_sems.at[1])
    settle_keep.start()

    all_sent(core_buf, sent_sems.at[0])

    @pl.when(stage < stages - 1)
    def _():
        all_sent(up_out, sent_sems.at[1])

    @pl.when(stage > 0)
    def _():
        all_sent(down_out, sent_sems.at[2])

    all_sent(taus.at[pl.ds(0, block - local_pairs)], sent_sems.at[3])
    for i in range(steps):
        mate_slab(i).wait_send()
    for j in range(pair_count - 1):
        all_sent(own_buf, sent_sems.at[4 + j])
    tile_taus = taus.at[pl.ds(0, block)]
    for d, shift in enumerate(shifts):
        @pl.when(in_range(shift))
        def _():
            all_sent(tile_taus, direct_sems.at[d])

    for source in range(stages):
        all_sent(tile_taus, mate_sent.at[source])

        @pl.when(jnp.logical_or(goes_up(source), goes_down(source)))
        def _():
            all_sent(tile_taus, relay_sems.at[source])

    settle_keep.wait()
    others = part.at[pl.ds(0, (total - 1) * local_pairs)]
    all_sent(others, settle_sems.at[0])
    all_sent(others, settle_sems.at[1])
    for z in range(stages):
        value = inbox[2 * z, 0]
        for tile_index in (2 * z, 2 * z + 1):
            for source in range(pair_count):
                if tile_index > 2 * z or source:
                    value += inbox[tile_index, source]
        res_ref[:, :, z * both_b : (z + 1) * both_b] = value


def settle_kernel(sum_ref, den_ref, res_ref, upd_ref):
    res_ref[...] = sum_ref[...]
    upd_ref[...] = sum_ref[...] / den_ref[...]


def settle(sums, den):
    shape = jax.ShapeDtypeStruct(sums.shape, F32)
    return pl.pallas_call(
        settle_kernel, out_shape=(shape, shape), in_specs=[VMEM, VMEM], out_specs=(VMEM, VMEM),
    )(sums, den)


def ladder(rows, turned, factors, pair_count, tile_count):
    window, cols, aux = rows.shape
    half = aux // 2
    own_b, own_d, _ = factors.shape
    local_pairs, virt, _ = turned.shape
    pairs = pair_count * tile_count * local_pairs
    both_b = 2 * own_b
    width = max(512, both_b)
    many = width // both_b
    sub = max(16, cols // 4)
    count = window * cols // sub
    steps = own_d // GROUP
    stages = tile_count // 2
    spread = GROUP * GROUP
    blocks = pairs // GROUP
    tile = min(1024, half)
    total = pair_count * tile_count
    kind = rows.dtype
    dma = pltpu.SemaphoreType.DMA
    piece = pltpu.VMEM((window, cols, half), kind)
    shape = jax.ShapeDtypeStruct((local_pairs, window, virt), F32)
    return pl.pallas_call(
        functools.partial(ladder_kernel, pair_count, tile_count, sub, width),
        out_shape=shape,
        in_specs=[VMEM, VMEM, HBM],
        out_specs=VMEM,
        scratch_shapes=[pltpu.VMEM((window, pair_count, cols, half), kind)]
        + [piece] * 6
        + [
            pltpu.VMEM((pairs, own_d, virt), kind),
            pltpu.VMEM((blocks, spread, virt), kind),
            pltpu.VMEM((2, steps, own_b, GROUP, half), kind),
            pltpu.VMEM((spread, spread), kind),
            pltpu.VMEM((GROUP // many, window, blocks, many * GROUP, tile), kind),
            pltpu.VMEM((window * blocks * many * GROUP, width), F32),
            pltpu.VMEM((pairs, window, both_b), F32),
            pltpu.VMEM((tile_count, pair_count, local_pairs, window, both_b), F32),
            dma((3 + pair_count,)), dma((count,)), dma((count,)), dma((count,)),
            dma((pair_count - 1, count)),
            dma((1,)), dma((4,)), dma((stages, steps)), dma((stages,)), dma((stages,)),
            dma((steps,)), dma((steps,)), dma((steps,)), dma((steps,)), dma((2,)), dma((2,)),
        ],
        compiler_params=pltpu.CompilerParams(
            collective_id=0, has_side_effects=True, vmem_limit_bytes=63 * 1024 * 1024
        ),
    )(rows, turned, factors)


def local(amplitudes, factors, pair_list, window_offsets, occupied_energy, virtual_energy):
    pair_count = lax.axis_size("pair")
    tile_count = lax.axis_size("vtile")
    rows, turned, den = prepare(
        amplitudes, factors, pair_list, window_offsets, occupied_energy, virtual_energy
    )
    sums = ladder(rows, turned, factors, pair_count, tile_count)
    return settle(sums, den)


def solution(mesh):
    return jax.shard_map(
        local,
        mesh=mesh,
        in_specs=(
            P(("pair", "vtile"), None, None),
            P("vtile", "pair", None),
            P(("pair", "vtile"), None),
            P(),
            P(),
            P(),
        ),
        out_specs=(P(("pair", "vtile"), None, None), P(("pair", "vtile"), None, None)),
        check_vma=False,
    )
```

```python
import functools

import jax
import jax.numpy as jnp
from jax import lax
from jax.experimental import pallas as pl
from jax.experimental.pallas import tpu as pltpu
from jax.sharding import PartitionSpec as P

MESH = pl.DeviceIdType.MESH
VMEM = pl.BlockSpec(memory_space=pltpu.VMEM)
SMEM = pl.BlockSpec(memory_space=pltpu.SMEM)
HBM = pl.BlockSpec(memory_space=pltpu.HBM)
F32 = jnp.float32
GROUP = 16
OWN_STEPS = (4, 6, 7, 8, 9, 10, 11)
RELAY_STEPS = (8, 10, 11)


def prepare_kernel(
    offsets_ref, pairs_ref, occupied_ref, energy_ref, virtual_ref, factors_ref, amp_ref,
    rows_ref, turned_ref, den_ref, sems,
):
    t = lax.axis_index("vtile")
    row_count = factors_ref.shape[0]
    window = rows_ref.shape[0]

    def local_row(k):
        return offsets_ref[k] - t * row_count

    def pick(k):
        row = jnp.clip(local_row(k), 0, row_count - 1)
        return pltpu.make_async_copy(factors_ref.at[row], rows_ref.at[k], sems.at[k])

    for k in range(window):
        pick(k).start()
    for pair in range(amp_ref.shape[0]):
        turned_ref[pair] = amp_ref[pair].T
        occupied = occupied_ref[pairs_ref[pair, 0]] + occupied_ref[pairs_ref[pair, 1]]
        for k in range(window):
            den_ref[pair, k : k + 1, :] = (energy_ref[offsets_ref[k]] + virtual_ref[...]) - occupied
    for k in range(window):
        pick(k).wait()
        row = local_row(k)

        @pl.when(jnp.logical_or(row < 0, row >= row_count))
        def _():
            rows_ref[k] = jnp.zeros(rows_ref.shape[1:], rows_ref.dtype)


def prepare(amplitudes, factors, pair_list, window_offsets, occupied_energy, virtual_energy):
    local_pairs, virt, _ = amplitudes.shape
    window = window_offsets.shape[0]
    return pl.pallas_call(
        prepare_kernel,
        out_shape=(
            jax.ShapeDtypeStruct((window,) + factors.shape[1:], factors.dtype),
            jax.ShapeDtypeStruct(amplitudes.shape, amplitudes.dtype),
            jax.ShapeDtypeStruct((local_pairs, window, virt), F32),
        ),
        in_specs=[SMEM, SMEM, SMEM, SMEM, VMEM, HBM, VMEM],
        out_specs=(VMEM, VMEM, VMEM),
        scratch_shapes=[pltpu.SemaphoreType.DMA((window,))],
    )(
        window_offsets, pair_list, occupied_energy, virtual_energy,
        virtual_energy.reshape(1, virt), factors, amplitudes,
    )


def ladder_kernel(
    pair_count, tile_count, sub, width,
    rows_ref, turned_ref, factors_ref,
    res_ref,
    full, core_buf, own_buf, up_buf, down_buf, up_out, down_out,
    taus, sorted_taus, table, swap, half_made, acc, part, inbox,
    sent_sems, core_sems, up_sems, down_sems, peer_sems,
    plane_sems, direct_sems, arrive_sems, relay_sems, mate_sent, mate_sems,
    slab_sent, slab_sems, load_sems, settle_sems, local_sems,
):
    p = lax.axis_index("pair")
    t = lax.axis_index("vtile")
    core = lax.rem(t, 2)
    stage = t // 2
    stages = tile_count // 2
    total = pair_count * tile_count
    me = p * tile_count + t
    window, cols, aux = rows_ref.shape
    half = aux // 2
    own_b, own_d, _ = factors_ref.shape
    both_b = 2 * own_b
    local_pairs = turned_ref.shape[0]
    block = pair_count * local_pairs
    pairs = tile_count * block
    steps = own_d // GROUP
    spread = swap.shape[0]
    mate = (p, stage * 2 + (1 - core))
    above = (p, t + 2)
    below = (p, t - 2)
    relayed = pair_count == 4
    if relayed:
        across = p + 1 - 2 * lax.rem(p, 2)
        along = lax.rem(p + 2, 4)
        sources = [across, along, lax.rem(across + 2, 4)]
        peers = [(source, t) for source in sources]
    else:
        peers = [(lax.rem(p + j, pair_count), t) for j in range(1, pair_count)]
        sources = [lax.rem(p + pair_count - j, pair_count) for j in range(1, pair_count)]
    near = 2 if relayed else pair_count - 1

    def place(offset):
        other = lax.rem(me + offset, total)
        return other // tile_count, lax.rem(other, tile_count)

    barrier = pltpu.get_barrier_semaphore()
    shifts = [shift for shift in (-2, -1, 1, 2) if abs(shift) < stages]

    def in_range(shift):
        return jnp.logical_and(stage + shift >= 0, stage + shift < stages)

    for device in [mate] + peers:
        pl.semaphore_signal(barrier, inc=1, device_id=device, device_id_type=MESH)
    expected = pair_count
    for shift in shifts:
        @pl.when(in_range(shift))
        def _():
            pl.semaphore_signal(
                barrier, inc=1, device_id=(p, t + 2 * shift), device_id_type=MESH
            )

        expected += in_range(shift).astype(jnp.int32)
    pl.semaphore_wait(barrier, expected)

    mine_lanes = pl.ds(pl.multiple_of(core * half, half), half)
    mate_lanes = pl.ds(pl.multiple_of((1 - core) * half, half), half)
    chunks = [(k, pl.ds(s * sub, sub)) for k in range(window) for s in range(cols // sub)]
    count = len(chunks)

    def remote(src, dst, sems, index, device):
        return pltpu.make_async_remote_copy(
            src_ref=src, dst_ref=dst, send_sem=sems[0], recv_sem=sems[1].at[index],
            device_id=device, device_id_type=MESH,
        )

    def all_sent(ref, sem):
        pltpu.make_async_remote_copy(
            src_ref=ref, dst_ref=ref, send_sem=sem, recv_sem=sem,
            device_id=mate, device_id_type=MESH,
        ).wait_recv()

    def group(i):
        return pl.ds(pl.multiple_of(i * GROUP, GROUP), GROUP)

    def core_copy(h):
        k, rows = chunks[h]
        return remote(rows_ref.at[k, rows, mate_lanes], core_buf.at[k, rows], (sent_sems.at[0], core_sems), (h,), mate)

    def up_copy(h):
        k, rows = chunks[h]
        return remote(up_out.at[k, rows], up_buf.at[k, rows], (sent_sems.at[1], up_sems), (h,), above)

    def down_copy(h):
        k, rows = chunks[h]
        return remote(down_out.at[k, rows], down_buf.at[k, rows], (sent_sems.at[2], down_sems), (h,), below)

    def peer_copy(h, j):
        k, rows = chunks[h]
        if j >= near:
            spot = full.at[k, sources[h % 2], rows]
            return remote(spot, spot, (sent_sems.at[4 + j], peer_sems), (j, h), peers[1 - h % 2])
        spot = full.at[k, p, rows]
        return remote(spot, spot, (sent_sems.at[4 + j], peer_sems), (j, h), peers[j])

    def plane_copy(j):
        there = peers[j][0]
        rows = pl.ds(pl.multiple_of(there * own_d, own_d), own_d)
        turn = lax.rem(p - there + pair_count, pair_count)
        spot = taus.at[pl.ds((t * pair_count + turn) * local_pairs, local_pairs)]
        return remote(turned_ref.at[:, rows], spot, (sent_sems.at[3], plane_sems), (0,), peers[j])

    def plane_keep():
        rows = pl.ds(pl.multiple_of(p * own_d, own_d), own_d)
        spot = taus.at[pl.ds(t * block, local_pairs)]
        return pltpu.make_async_copy(turned_ref.at[:, rows], spot, local_sems.at[0])

    def tau_spot(tile, i):
        return taus.at[pl.ds(tile * block, block), group(i)]

    def direct_copy(d, i):
        return pltpu.make_async_remote_copy(
            src_ref=tau_spot(t, i), dst_ref=tau_spot(t, i),
            send_sem=direct_sems.at[d], recv_sem=arrive_sems.at[stage, i],
            device_id=(p, t + 2 * shifts[d]), device_id_type=MESH,
        )

    def relay_copy(source, i, shift):
        spot = tau_spot(2 * source + core, i)
        return pltpu.make_async_remote_copy(
            src_ref=spot, dst_ref=spot,
            send_sem=relay_sems.at[source], recv_sem=arrive_sems.at[source, i],
            device_id=(p, t + 2 * shift), device_id_type=MESH,
        )

    def mate_copy(source, i):
        spot = tau_spot(2 * source + core, i)
        return remote(spot, spot, (mate_sent.at[source], mate_sems), (i,), mate)

    def goes_up(source):
        return jnp.logical_and(stage >= source + 2, stage + 1 < stages)

    def goes_down(source):
        return jnp.logical_and(stage <= source - 2, stage >= 1)

    def mate_wait(i):
        all_sent(taus.at[pl.ds(0, stages * block), group(i)], mate_sems.at[i])

    def send_own(i):
        for d, shift in enumerate(shifts):
            @pl.when(in_range(shift))
            def _():
                direct_copy(d, i).start()

    def relay(i):
        for source in range(stages):
            @pl.when(goes_up(source))
            def _():
                relay_copy(source, i, 1).wait_recv()
                relay_copy(source, i, 1).start()

            @pl.when(goes_down(source))
            def _():
                relay_copy(source, i, -1).wait_recv()
                relay_copy(source, i, -1).start()

    def collect(i):
        for source in range(stages):
            passed = jnp.logical_or(goes_up(source), goes_down(source))

            @pl.when(jnp.logical_not(jnp.logical_or(passed, stage == source)))
            def _():
                relay_copy(source, i, 1).wait_recv()

            mate_copy(source, i).start()

    def mate_slab(i):
        return remote(factors_ref.at[:, group(i), mate_lanes], table.at[core, i], (slab_sent.at[i], slab_sems), (i,), mate)

    def own_slab(i):
        return pltpu.make_async_copy(
            factors_ref.at[:, group(i), mine_lanes], table.at[core, i], load_sems.at[i]
        )

    def sort_slab(side, i):
        def one(b, carry):
            rows = table[side, i, group(b)].reshape(spread, half)
            made = jnp.dot(swap[...], rows, preferred_element_type=F32).astype(table.dtype)
            table[side, i, group(b)] = made.reshape(GROUP, GROUP, half)
            return carry

        lax.fori_loop(0, own_b // GROUP, one, 0)

    def finish_slab(n):
        if n < steps:
            own_slab(n).wait()
            sort_slab(core, n)
        else:
            mate_slab(n - steps).wait_recv()
            sort_slab(1 - core, n - steps)

    slabs = 2 * steps
    own_steps = dict(zip(OWN_STEPS, range(steps)))
    relay_steps = dict(zip(RELAY_STEPS, range(steps)))
    relays = len(relay_steps)
    sends = len(own_steps)

    for h in range(count):
        core_copy(h).start()
    for j in range(pair_count - 1):
        plane_copy(j).start()
    plane_keep().start()
    for i in range(steps):
        own_slab(i).start()
        mate_slab(i).start()
    lanes = lax.broadcasted_iota(jnp.int32, (spread, spread), 1)
    lines = lax.broadcasted_iota(jnp.int32, (spread, spread), 0)
    swap[...] = jnp.where(
        jnp.logical_and(lines // GROUP == lanes % GROUP, lines % GROUP == lanes // GROUP), 1.0, 0.0
    ).astype(swap.dtype)
    acc[...] = jnp.zeros_like(acc)

    def combine(h):
        k, rows = chunks[h]
        core_copy(h).wait_recv()
        own_buf[k, rows, :] = rows_ref[k, rows, mine_lanes] + core_buf[k, rows, :]

        @pl.when(stage == 0)
        def _():
            up_out[k, rows, :] = own_buf[k, rows, :]
            up_copy(h).start()

        @pl.when(stage == stages - 1)
        def _():
            down_out[k, rows, :] = own_buf[k, rows, :]
            down_copy(h).start()

    def go_up(h):
        k, rows = chunks[h]

        @pl.when(stage > 0)
        def _():
            up_copy(h).wait_recv()

            @pl.when(stage < stages - 1)
            def _():
                up_out[k, rows, :] = own_buf[k, rows, :] + up_buf[k, rows, :]
                up_copy(h).start()

    def go_down(h):
        k, rows = chunks[h]

        @pl.when(stage < stages - 1)
        def _():
            down_copy(h).wait_recv()

            @pl.when(stage > 0)
            def _():
                down_out[k, rows, :] = own_buf[k, rows, :] + down_buf[k, rows, :]
                down_copy(h).start()

    def finish(h):
        k, rows = chunks[h]

        @pl.when(stage == 0)
        def _():
            full[k, p, rows, :] = own_buf[k, rows, :] + down_buf[k, rows, :]

        @pl.when(stage == stages - 1)
        def _():
            full[k, p, rows, :] = own_buf[k, rows, :] + up_buf[k, rows, :]

        @pl.when(jnp.logical_and(stage > 0, stage < stages - 1))
        def _():
            full[k, p, rows, :] = own_buf[k, rows, :] + up_buf[k, rows, :] + down_buf[k, rows, :]

        for j in range(near):
            peer_copy(h, j).start()

    def forward(h):
        for j in range(near):
            peer_copy(h, j).wait_recv()
            if relayed and j == h % 2:
                peer_copy(h, near).start()

    def forward_far(h):
        for j in range(near, pair_count - 1):
            peer_copy(h, j).wait_recv()

    lower = stage < stages // 2
    ahead, lag = 2, 2

    def early(h):
        @pl.when(lower)
        def _():
            go_up(h)

        @pl.when(jnp.logical_not(lower))
        def _():
            go_down(h)

    def late(h):
        @pl.when(lower)
        def _():
            go_down(h)

        @pl.when(jnp.logical_not(lower))
        def _():
            go_up(h)

    for h in range(count):
        combine(h)
    sorted_count = 0
    for step in range(-ahead, count + 2 * lag):
        if 0 <= step + ahead < count:
            early(step + ahead)
        if 0 <= step < count:
            late(step)
            finish(step)
        if 0 <= step - lag < count:
            forward(step - lag)
        if 0 <= step - 2 * lag < count:
            forward_far(step - 2 * lag)
        if step == 0:
            all_sent(taus.at[pl.ds(t * block + local_pairs, block - local_pairs)], plane_sems.at[0])
            plane_keep().wait()
        if step in own_steps:
            send_own(own_steps[step])
        if step in relay_steps:
            relay(relay_steps[step])
        if sorted_count < slabs:
            finish_slab(sorted_count)
            sorted_count += 1
    while sorted_count < slabs:
        finish_slab(sorted_count)
        sorted_count += 1
    for i in range(relays, min(2, steps)):
        relay(i)
    collect(0)

    blocks = pairs // GROUP
    many = width // both_b
    tile = half_made.shape[-1]

    def main(i, carry):
        @pl.when(i + sends < steps)
        def _():
            send_own(i + sends)

        mate_wait(i)

        @pl.when(jnp.logical_and(i + 2 >= relays, i + 2 < steps))
        def _():
            relay(i + 2)

        for s in range(blocks):
            rows = taus[s * GROUP : (s + 1) * GROUP, group(i), :].reshape(spread, -1)
            sorted_taus[s] = jnp.dot(swap[...], rows, preferred_element_type=F32).astype(taus.dtype)
        left = sorted_taus[...].reshape(blocks * spread, -1)

        def part_of(j, inner):
            qs = pl.ds(pl.multiple_of(j * tile, tile), tile)
            for k in range(window):
                right = full[k, :, :, qs].reshape(pair_count * cols, tile)
                made = jnp.dot(left, right, preferred_element_type=F32).astype(half_made.dtype)
                made = made.reshape(blocks, GROUP // many, many * GROUP, tile)
                for u in range(GROUP // many):
                    half_made[u, k] = made[:, u]

            @pl.when(jnp.logical_and(j == 0, i + 1 < steps))
            def _():
                collect(i + 1)

            added = acc[...]
            for u in range(GROUP // many):
                right = jnp.concatenate(
                    [
                        table[side, i, b + u * many : b + (u + 1) * many, :, qs].reshape(-1, tile)
                        for side in range(2)
                        for b in range(0, own_b, GROUP)
                    ]
                )
                added += lax.dot_general(
                    half_made[u].reshape(-1, tile), right, (((1,), (1,)), ((), ())),
                    preferred_element_type=F32,
                )
            acc[...] = added
            return inner

        lax.fori_loop(0, half // tile, part_of, 0)

        return carry

    lax.fori_loop(0, steps, main, 0)

    lines = lax.broadcasted_iota(jnp.int32, (width, both_b), 0)
    lanes = lax.broadcasted_iota(jnp.int32, (width, both_b), 1)
    same_block = lines // (many * GROUP) == lanes // GROUP
    choose = jnp.where(jnp.logical_and(same_block, lines % GROUP == lanes % GROUP), 1.0, 0.0)
    which = lax.broadcasted_iota(jnp.int32, (GROUP, width), 1) // GROUP % many
    for k in range(window):
        for s in range(blocks):
            base = (k * blocks + s) * many * GROUP
            value = jnp.where(which == 0, acc[base : base + GROUP, :], 0.0)
            for u in range(1, many):
                rows = acc[base + u * GROUP : base + (u + 1) * GROUP, :]
                value += jnp.where(which == u, rows, 0.0)
            part[s * GROUP : (s + 1) * GROUP, k, :] = jnp.dot(
                value, choose, precision=lax.Precision.HIGHEST, preferred_element_type=F32
            )

    def settle_copy(offset):
        there = place(offset)
        turn = lax.rem(there[0] - p + pair_count, pair_count)
        spot = pl.ds((there[1] * pair_count + turn) * local_pairs, local_pairs)
        return pltpu.make_async_remote_copy(
            src_ref=part.at[spot], dst_ref=inbox.at[t, p],
            send_sem=settle_sems.at[0], recv_sem=settle_sems.at[1],
            device_id=there, device_id_type=MESH,
        )

    for offset in range(1, total):
        settle_copy(offset).start()
    spot = pl.ds(t * block, local_pairs)
    settle_keep = pltpu.make_async_copy(part.at[spot], inbox.at[t, p], local_sems.at[1])
    settle_keep.start()

    all_sent(core_buf, sent_sems.at[0])

    @pl.when(stage < stages - 1)
    def _():
        all_sent(up_out, sent_sems.at[1])

    @pl.when(stage > 0)
    def _():
        all_sent(down_out, sent_sems.at[2])

    all_sent(taus.at[pl.ds(0, block - local_pairs)], sent_sems.at[3])
    for i in range(steps):
        mate_slab(i).wait_send()
    for j in range(pair_count - 1):
        all_sent(own_buf, sent_sems.at[4 + j])
    tile_taus = taus.at[pl.ds(0, block)]
    for d, shift in enumerate(shifts):
        @pl.when(in_range(shift))
        def _():
            all_sent(tile_taus, direct_sems.at[d])

    for source in range(stages):
        all_sent(tile_taus, mate_sent.at[source])

        @pl.when(jnp.logical_or(goes_up(source), goes_down(source)))
        def _():
            all_sent(tile_taus, relay_sems.at[source])

    settle_keep.wait()
    others = part.at[pl.ds(0, (total - 1) * local_pairs)]
    all_sent(others, settle_sems.at[0])
    all_sent(others, settle_sems.at[1])
    for z in range(stages):
        value = inbox[2 * z, 0]
        for tile_index in (2 * z, 2 * z + 1):
            for source in range(pair_count):
                if tile_index > 2 * z or source:
                    value += inbox[tile_index, source]
        res_ref[:, :, z * both_b : (z + 1) * both_b] = value


def settle_kernel(sum_ref, den_ref, res_ref, upd_ref):
    res_ref[...] = sum_ref[...]
    upd_ref[...] = sum_ref[...] / den_ref[...]


def settle(sums, den):
    shape = jax.ShapeDtypeStruct(sums.shape, F32)
    return pl.pallas_call(
        settle_kernel, out_shape=(shape, shape), in_specs=[VMEM, VMEM], out_specs=(VMEM, VMEM),
    )(sums, den)


def ladder(rows, turned, factors, pair_count, tile_count):
    window, cols, aux = rows.shape
    half = aux // 2
    own_b, own_d, _ = factors.shape
    local_pairs, virt, _ = turned.shape
    pairs = pair_count * tile_count * local_pairs
    both_b = 2 * own_b
    width = max(512, both_b)
    many = width // both_b
    sub = max(16, cols // 4)
    count = window * cols // sub
    steps = own_d // GROUP
    stages = tile_count // 2
    spread = GROUP * GROUP
    blocks = pairs // GROUP
    tile = min(1024, half)
    total = pair_count * tile_count
    kind = rows.dtype
    dma = pltpu.SemaphoreType.DMA
    piece = pltpu.VMEM((window, cols, half), kind)
    shape = jax.ShapeDtypeStruct((local_pairs, window, virt), F32)
    return pl.pallas_call(
        functools.partial(ladder_kernel, pair_count, tile_count, sub, width),
        out_shape=shape,
        in_specs=[VMEM, VMEM, HBM],
        out_specs=VMEM,
        scratch_shapes=[pltpu.VMEM((window, pair_count, cols, half), kind)]
        + [piece] * 6
        + [
            pltpu.VMEM((pairs, own_d, virt), kind),
            pltpu.VMEM((blocks, spread, virt), kind),
            pltpu.VMEM((2, steps, own_b, GROUP, half), kind),
            pltpu.VMEM((spread, spread), kind),
            pltpu.VMEM((GROUP // many, window, blocks, many * GROUP, tile), kind),
            pltpu.VMEM((window * blocks * many * GROUP, width), F32),
            pltpu.VMEM((pairs, window, both_b), F32),
            pltpu.VMEM((tile_count, pair_count, local_pairs, window, both_b), F32),
            dma((3 + pair_count,)), dma((count,)), dma((count,)), dma((count,)),
            dma((pair_count - 1, count)),
            dma((1,)), dma((4,)), dma((stages, steps)), dma((stages,)), dma((stages,)),
            dma((steps,)), dma((steps,)), dma((steps,)), dma((steps,)), dma((2,)), dma((2,)),
        ],
        compiler_params=pltpu.CompilerParams(
            collective_id=0, has_side_effects=True, vmem_limit_bytes=63 * 1024 * 1024
        ),
    )(rows, turned, factors)


def local(amplitudes, factors, pair_list, window_offsets, occupied_energy, virtual_energy):
    pair_count = lax.axis_size("pair")
    tile_count = lax.axis_size("vtile")
    rows, turned, den = prepare(
        amplitudes, factors, pair_list, window_offsets, occupied_energy, virtual_energy
    )
    sums = ladder(rows, turned, factors, pair_count, tile_count)
    return settle(sums, den)


def solution(mesh):
    return jax.shard_map(
        local,
        mesh=mesh,
        in_specs=(
            P(("pair", "vtile"), None, None),
            P("vtile", "pair", None),
            P(("pair", "vtile"), None),
            P(),
            P(),
            P(),
        ),
        out_specs=(P(("pair", "vtile"), None, None), P(("pair", "vtile"), None, None)),
        check_vma=False,
    )
```
